32 devices in a mesh: rep: 8 (over y, x, core), fsdp: 4 (over z).
Axes of the slice: x: 2, y: 2, z: 4, core: 2. Of those that a mesh axis runs over, the one named last changes fastest.
Arguments:
- latents: float32 [2, 32, 320, 256], P(None, ('rep', 'fsdp')), may hold values from -6 to 6
- gaussian: float32 [2, 32, 320, 256], P(None, ('rep', 'fsdp')), may hold values from -6 to 6
- stamps: int32 [2, 32], P(None, ('rep', 'fsdp')), may hold values from 0 to 999
- numerator: float32 [8, 320, 2880], P('rep', 'fsdp'), may hold values from -6 to 6
- momentum: float32 [8, 320, 2880], P('rep', 'fsdp'), may hold values from -1.5 to 1.5
- push_weight: float32 [8], P('rep'), may hold values from 0.5 to 2
- arrived_numerator: float32 [8, 320, 2880], P('rep', 'fsdp'), may hold values from -6 to 6
- arrived_weight: float32 [8], P('rep'), may hold values from 0.25 to 1
Outputs:
- numerator_out: float32 [8, 320, 2880], P('rep', 'fsdp')
- momentum_out: float32 [8, 320, 2880], P('rep', 'fsdp')
- weight_out: float32 [8], P('rep')
- pending_numerator: float32 [8, 320, 2880], P('rep', 'fsdp')
- pending_weight: float32 [8], P('rep')
The draws below stay inside these ranges and needn't reach their ends.
All inputs are finite; a program needn't handle non-finite values.
Results may differ from the reference program's by a relative error of at most 0.0003.
Values sent between devices are 32-bit elements; how exact they have to be, the bound alone decides.
A program may use at most 64 MiB of HBM per device.

```python
import math
import jax
import jax.numpy as jnp
from jax import lax

C = 320
GROUPS = 32
CROP_H = 16
CROP_W = 16
STEPS = 2
TRAIN_T = 1000
PIX = 256
KKC = 2880
REPS = 8
BATCH = 32


def touch_ends(array, stream_key, smallest, largest):
    longest = array.shape.index(max(array.shape))
    spots = []
    for shift in (0, 1):
        where = [jax.random.randint(jax.random.fold_in(stream_key, axis), (), 0, length) for axis, length in enumerate(array.shape)]
        where[longest] = (where[longest] + shift) % array.shape[longest]
        spots.append(tuple(where))
    return array.at[spots[0]].set(smallest).at[spots[1]].set(largest)


def block_scale(rng, shape, pieces, low, top_value):
    def one(dim, shards_of):
        steps = jax.random.uniform(jax.random.fold_in(jax.random.fold_in(rng, 6), dim), (shards_of,), jnp.float32, low / len(pieces), top_value / len(pieces))
        return jnp.repeat(jnp.exp(steps), shape[dim] // shards_of).reshape((-1,) + (1,) * (len(shape) - dim - 1))

    factor_of = one(*pieces[0])
    for cut in pieces[1:]:
        factor_of = factor_of * one(*cut)
    return factor_of


def noise(rng, extent, width, bound, cuts=(), kind=jnp.bfloat16):
    array = width * jax.random.normal(rng, extent, jnp.float32)
    if cuts:
        array = array * block_scale(rng, extent, cuts, -0.22, 0.18)
    return jnp.clip(array, -bound, bound).astype(kind)


def setup_inputs(seed: int = 0) -> dict:
    keys = jax.random.split(jax.random.key(seed), 9)
    return {
        "latents": noise(keys[0], (STEPS, BATCH, C, PIX), 1.0, 6.0, ((1, 32),), jnp.float32),
        "gaussian": noise(keys[1], (STEPS, BATCH, C, PIX), 1.0, 6.0, ((1, 32),), jnp.float32),
        "stamps": touch_ends(jax.random.randint(keys[2], (STEPS, BATCH), 0, TRAIN_T), jax.random.fold_in(keys[2], 1), 0, TRAIN_T - 1).astype(jnp.int32),
        "numerator": noise(keys[3], (REPS, C, KKC), 1.0, 6.0, ((0, 8), (1, 4)), jnp.float32),
        "momentum": noise(keys[4], (REPS, C, KKC), 0.1, 1.5, ((0, 8), (1, 4)), jnp.float32),
        "push_weight": jnp.clip(jnp.exp(math.log(2.0) - 1.3862944 * jax.random.uniform(keys[5], (REPS,), jnp.float32) ** block_scale(keys[5], (REPS,), ((0, 8),), -0.2, 0.2)), 0.5, 2.0),
        "arrived_numerator": noise(keys[6], (REPS, C, KKC), 0.5, 6.0, ((0, 8), (1, 4)), jnp.float32),
        "arrived_weight": jnp.clip(jnp.exp(math.log(1.0) - 1.3862944 * jax.random.uniform(keys[7], (REPS,), jnp.float32) ** block_scale(keys[7], (REPS,), ((0, 8),), -0.2, 0.2)), 0.25, 1.0),
    }


norm_epsilon = 1e-05
momentum_decay = 0.9
step_size = 1.0
beta_first = 0.00085
beta_last = 0.012
highest = lax.Precision.HIGHEST

def noise_levels(stamps):
    fraction = jnp.arange(TRAIN_T, dtype=jnp.float32) / (TRAIN_T - 1)
    root_first = beta_first ** 0.5
    root_last = beta_last ** 0.5
    beta_values = jnp.square(root_first + fraction * (root_last - root_first))
    cumulative = jnp.cumprod(1.0 - beta_values)
    matches = stamps[..., None] == jnp.arange(TRAIN_T, dtype=jnp.int32)
    return lax.optimization_barrier(jnp.sum(jnp.where(matches, cumulative, jnp.float32(0.0)), axis=-1))

def activations(latents, gaussian, stamps):
    levels = noise_levels(stamps)[:, None, None]
    noised = jnp.sqrt(levels) * latents + jnp.sqrt(1.0 - levels) * gaussian
    samples, channels, pixels = noised.shape
    grouped = noised.reshape(samples, GROUPS, channels // GROUPS, pixels)
    center = lax.optimization_barrier(jnp.mean(grouped, axis=(2, 3), keepdims=True))
    spread = lax.optimization_barrier(jnp.mean(jnp.square(grouped - center), axis=(2, 3), keepdims=True))
    normed = ((grouped - center) * lax.rsqrt(spread + norm_epsilon)).reshape(samples, channels, pixels)
    return (jax.nn.silu(normed), noised - gaussian)

def unfold_taps(signal):
    samples, channels, pixels = signal.shape
    picture = signal.reshape(samples, channels, CROP_H, CROP_W)
    padded = jnp.pad(picture, ((0, 0), (0, 0), (1, 1), (1, 1)))
    shifted = [padded[:, :, row_shift:row_shift + CROP_H, col_shift:col_shift + CROP_W] for row_shift in range(3) for col_shift in range(3)]
    return jnp.stack(shifted, axis=1).reshape(samples, 9 * channels, pixels)

def replica_gradient(kernel, latents, gaussian, stamps):
    hidden_acts, target_gap = activations(latents, gaussian, stamps)
    unfolded = unfold_taps(hidden_acts)
    tap_scale = kernel.shape[1] ** (-0.5)
    output = jnp.einsum('oj,bjp->bop', kernel, unfolded, precision=highest)
    residual = target_gap + tap_scale * output
    summed = jnp.einsum('bop,bjp->oj', residual, unfolded, precision=highest)
    return summed * (tap_scale / latents.shape[0])

def reference(latents, gaussian, stamps, numerator, momentum, push_weight, arrived_numerator, arrived_weight):
    replicas = numerator.shape[0]
    per_replica = latents.shape[1] // replicas
    split_latents = latents.reshape(latents.shape[0], replicas, per_replica, latents.shape[2], latents.shape[3])
    split_gaussian = gaussian.reshape(gaussian.shape[0], replicas, per_replica, gaussian.shape[2], gaussian.shape[3])
    split_stamps = stamps.reshape(stamps.shape[0], replicas, per_replica)

    def one_replica(bundle):
        return replica_gradient(bundle[0], bundle[1], bundle[2], bundle[3])
    for step_index in range(STEPS):
        kernel = numerator / push_weight[:, None, None]
        gradient = lax.map(one_replica, (kernel, split_latents[step_index], split_gaussian[step_index], split_stamps[step_index]))
        momentum = momentum_decay * momentum + gradient
        moved = numerator - step_size * momentum
        numerator = 0.5 * moved + arrived_numerator
        sent_weight = 0.5 * push_weight
        push_weight = sent_weight + arrived_weight
        distance = 2 ** step_index
        arrived_numerator = jnp.roll(0.5 * moved, distance, axis=0)
        arrived_weight = jnp.roll(sent_weight, distance, axis=0)
    return (numerator, momentum, push_weight, arrived_numerator, arrived_weight)
```

```python
import functools

import jax
import jax.numpy as jnp
from jax import lax
from jax.experimental import pallas as pl
from jax.experimental.pallas import tpu as pltpu
from jax.sharding import PartitionSpec as P

GROUPS = 32
CROP_H = 16
CROP_W = 16
STEPS = 2
TRAIN_T = 1000
TAPS = 9

norm_epsilon = 1e-05
momentum_decay = 0.9
step_size = 1.0
beta_first = 0.00085
beta_last = 0.012
MESH = pl.DeviceIdType.MESH


def split(value):
    high = value.astype(jnp.bfloat16)
    return high, (value - high.astype(jnp.float32)).astype(jnp.bfloat16)


def product(a, b, contract):
    dims = ((contract[0], contract[1]), ((), ()))
    dot = functools.partial(
        lax.dot_general, dimension_numbers=dims, preferred_element_type=jnp.float32
    )
    return dot(a[0], b[0]) + (dot(a[0], b[1]) + dot(a[1], b[0]))


def noise_level(stamp):
    rows = -(-TRAIN_T // 128)
    shape = (rows, 128)
    position = lax.broadcasted_iota(jnp.int32, shape, 0) * 128 + lax.broadcasted_iota(
        jnp.int32, shape, 1
    )
    fraction = position.astype(jnp.float32) / (TRAIN_T - 1)
    root_first = beta_first**0.5
    root_last = beta_last**0.5
    root = root_first + fraction * (root_last - root_first)
    factor = jnp.where(position <= stamp, 1.0 - root * root, jnp.float32(1.0))
    for shift in (64, 32, 16, 8, 4, 2, 1):
        factor = factor * pltpu.roll(factor, shift, 1)
    for shift in (4, 2, 1):
        factor = factor * pltpu.roll(factor, shift, 0)
    return factor


def group_mean(value, same_group, count):
    row = jnp.sum(value, axis=1, keepdims=True)
    row = jnp.broadcast_to(row, (row.shape[0], 128))
    first = row.astype(jnp.bfloat16)
    rest = row - first.astype(jnp.float32)
    second = rest.astype(jnp.bfloat16)
    third = (rest - second.astype(jnp.float32)).astype(jnp.bfloat16)
    dot = functools.partial(jnp.dot, preferred_element_type=jnp.float32)
    total = dot(same_group, first) + (dot(same_group, second) + dot(same_group, third))
    return total[:, 0:1] * (1.0 / count)


def tap_shift(tap):
    return (tap // 3 - 1) * CROP_W + (tap % 3 - 1)


def tap_mask(tap, pixels):
    place = lax.broadcasted_iota(jnp.int32, (1, pixels), 1)
    row = place // CROP_W + (tap // 3 - 1)
    col = place % CROP_W + (tap % 3 - 1)
    return (row >= 0) & (row < CROP_H) & (col >= 0) & (col < CROP_W)


def body(
    sizes,
    stamps, latents, gaussian, numerator, momentum, weight, arrived, arrived_weight,
    numerator_out, momentum_out, weight_out, pending_out, pending_weight_out,
    acts, gap_own, gap_rows, kernel_hi, kernel_lo, res_hi, res_lo, total, taps_out,
    outbox, inbox, weight_box,
    acts_send, acts_recv, gap_send, gap_recv, push_send, push_recv, weight_send, weight_recv,
):
    reps, shards, padded, chunk = sizes
    rows, columns = numerator.shape
    channels, pixels = latents.shape[1:]
    replica_batch = shards
    tap_scale = columns ** (-0.5)
    rep = lax.axis_index("rep")
    me = lax.axis_index("fsdp")

    offsets = sorted({2**k % reps for k in range(STEPS)} | {-(2**k) % reps for k in range(STEPS)})
    barrier = pltpu.get_barrier_semaphore()
    for offset in range(1, shards):
        pl.semaphore_signal(
            barrier, inc=1, device_id={"fsdp": lax.rem(me + offset, shards)}, device_id_type=MESH
        )
    for offset in offsets:
        pl.semaphore_signal(
            barrier, inc=1, device_id={"rep": lax.rem(rep + offset, reps)}, device_id_type=MESH
        )

    def acts_copy(step, owner, right):
        side = 1 if right else 0
        return pltpu.make_async_remote_copy(
            src_ref=acts.at[step, owner],
            dst_ref=acts.at[step, owner],
            send_sem=acts_send.at[side, step, owner],
            recv_sem=acts_recv.at[step, owner],
            device_id={"fsdp": me + 1 if right else me - 1},
            device_id_type=MESH,
        )

    def gap_copy(step, target):
        return pltpu.make_async_remote_copy(
            src_ref=gap_own.at[step, target],
            dst_ref=gap_rows.at[step, me],
            send_sem=gap_send.at[step, target],
            recv_sem=gap_recv.at[step, me],
            device_id={"fsdp": target},
            device_id_type=MESH,
        )

    def gap_arrival(step, owner):
        return pltpu.make_async_remote_copy(
            src_ref=gap_own.at[step, owner],
            dst_ref=gap_rows.at[step, owner],
            send_sem=gap_send.at[step, owner],
            recv_sem=gap_recv.at[step, owner],
            device_id={"fsdp": owner},
            device_id_type=MESH,
        )

    def push_copy(step, part):
        span = pl.ds(part * chunk, chunk)
        target = (inbox if step < STEPS - 1 else pending_out).at[span]
        return pltpu.make_async_remote_copy(
            src_ref=outbox.at[step, span],
            dst_ref=target,
            send_sem=push_send.at[step, part],
            recv_sem=push_recv.at[step, part],
            device_id={"rep": lax.rem(rep + 2**step, reps)},
            device_id_type=MESH,
        )

    def weight_copy(step):
        return pltpu.make_async_remote_copy(
            src_ref=weight_box.at[0, step],
            dst_ref=weight_box.at[1, step],
            send_sem=weight_send.at[step],
            recv_sem=weight_recv.at[step],
            device_id={"rep": lax.rem(rep + 2**step, reps)},
            device_id_type=MESH,
        )

    def send_own(step, right):
        @pl.when(me < shards - 1 if right else me > 0)
        def _():
            acts_copy(step, me, right).start()
            for away in range(1, shards):
                target = me + away if right else me - away

                @pl.when(target < shards if right else target >= 0)
                def _():
                    gap_copy(step, target).start()

    same_group = (
        lax.broadcasted_iota(jnp.int32, (channels, channels), 0) // (channels // GROUPS)
        == lax.broadcasted_iota(jnp.int32, (channels, channels), 1) // (channels // GROUPS)
    ).astype(jnp.float32).astype(jnp.bfloat16)
    count = (channels // GROUPS) * pixels

    def activate(step):
        level = noise_level(stamps[step, 0])[0:1, 0:1]
        noise = gaussian[step]
        noised = jnp.sqrt(level) * latents[step] + jnp.sqrt(1.0 - level) * noise
        gap = noised - noise
        for target in range(shards):
            gap_own[step, target] = gap[target * rows : (target + 1) * rows]
        centered = noised - group_mean(noised, same_group, count)
        spread = group_mean(centered * centered, same_group, count)
        normed = centered * lax.rsqrt(spread + norm_epsilon)
        acts[step, me] = normed / (1.0 + jnp.exp(-normed))
        gap_rows[step, me] = gap_own[step, me]

    activate(0)
    first_weight = jnp.broadcast_to(weight[...], weight_box.shape[2:])
    weight_box[0, 0] = 0.5 * first_weight
    second_weight = 0.5 * first_weight + jnp.broadcast_to(
        arrived_weight[...], weight_box.shape[2:]
    )
    weight_box[0, 1] = 0.5 * second_weight
    pl.semaphore_wait(barrier, shards - 1 + len(offsets))
    send_own(0, True)
    send_own(0, False)
    for step in range(STEPS):
        weight_copy(step).start()
    for step in range(1, STEPS):
        activate(step)

    @pl.when(me == 0)
    def _():
        for step in range(1, STEPS):
            send_own(step, True)

    @pl.when(me == shards - 1)
    def _():
        for step in range(1, STEPS):
            send_own(step, False)

    if padded != rows:
        for ref in (kernel_hi, kernel_lo, res_hi, res_lo):
            ref[...] = jnp.zeros(ref.shape, ref.dtype)

    def set_kernel(tap, first, values):
        high, low = split(values)
        start = tap * padded + first
        kernel_hi[start : start + values.shape[0]] = high
        kernel_lo[start : start + values.shape[0]] = low

    for tap in range(TAPS):
        set_kernel(
            tap, 0, numerator[:, tap * channels : (tap + 1) * channels] / first_weight[0:1, 0:1]
        )

    def process(step, owner):
        signal = split(acts[step, owner])
        taps_out[...] = product((kernel_hi[...], kernel_lo[...]), signal, ((1,), (0,)))
        output = jnp.zeros((rows, pixels), jnp.float32)
        for tap in range(TAPS):
            value = taps_out[tap * padded : tap * padded + rows]
            moved = pltpu.roll(value, -tap_shift(tap) % pixels, 1) if tap_shift(tap) else value
            output += jnp.where(tap_mask(tap, pixels), moved, 0.0)
        residual = gap_rows[step, owner] + tap_scale * output
        for tap in range(TAPS):
            value = jnp.where(tap_mask(tap, pixels), residual, 0.0)
            if tap_shift(tap):
                value = pltpu.roll(value, tap_shift(tap) % pixels, 1)
            high, low = split(value)
            res_hi[tap * padded : tap * padded + rows] = high
            res_lo[tap * padded : tap * padded + rows] = low
        total[...] += product((res_hi[...], res_lo[...]), signal, ((1,), (1,)))

    for step in range(STEPS):
        total[...] = jnp.zeros(total.shape, jnp.float32)

        def visit(k, _, step=step):
            away = (k + 1) // 2
            owner = jnp.where(lax.rem(k, 2) == 1, me - away, me + away)

            @pl.when((owner >= 0) & (owner < shards))
            def _():
                @pl.when(owner < me)
                def _():
                    acts_copy(step, owner, True).wait_recv()

                    @pl.when(me < shards - 1)
                    def _():
                        acts_copy(step, owner, True).start()

                    if step < STEPS - 1:

                        @pl.when(owner == 0)
                        def _():
                            send_own(step + 1, True)

                @pl.when(owner > me)
                def _():
                    acts_copy(step, owner, False).wait_recv()

                    @pl.when(me > 0)
                    def _():
                        acts_copy(step, owner, False).start()

                    if step < STEPS - 1:

                        @pl.when(owner == shards - 1)
                        def _():
                            send_own(step + 1, False)

                @pl.when(owner != me)
                def _():
                    gap_arrival(step, owner).wait_recv()

                process(step, owner)

            return 0

        lax.fori_loop(0, 2 * shards - 1, visit, 0)

        if step > 0:
            for part in range(rows // chunk):
                push_copy(step - 1, part).wait_recv()
        for part in range(rows // chunk):
            span = slice(part * chunk, (part + 1) * chunk)
            for tap in range(TAPS):
                cut = slice(tap * channels, (tap + 1) * channels)
                start = tap * padded + part * chunk
                gradient = total[start : start + chunk] * (tap_scale / replica_batch)
                old = (momentum if step == 0 else momentum_out)[span, cut]
                new = momentum_decay * old + gradient
                momentum_out[span, cut] = new
                base = (numerator if step == 0 else numerator_out)[span, cut]
                half = 0.5 * (base - step_size * new)
                outbox[step, span, cut] = half
                fresh = half + (arrived if step == 0 else inbox)[span, cut]
                numerator_out[span, cut] = fresh
                if step < STEPS - 1:
                    set_kernel(tap, part * chunk, fresh / second_weight[0:1, 0:1])
            push_copy(step, part).start()

    for step in range(STEPS):
        weight_copy(step).wait_recv()
    weight_out[...] = (0.5 * second_weight + weight_box[1, 0])[0:1, 0:1]
    pending_weight_out[...] = weight_box[1, 1][0:1, 0:1]
    for step in range(STEPS):
        weight_copy(step).wait_send()
        for part in range(rows // chunk):
            push_copy(step, part).wait_send()
            if step == STEPS - 1:
                push_copy(step, part).wait_recv()

        def drain(owner, _, step=step):
            @pl.when((owner <= me) & (me < shards - 1))
            def _():
                acts_copy(step, owner, True).wait_send()

            @pl.when((owner >= me) & (me > 0))
            def _():
                acts_copy(step, owner, False).wait_send()

            @pl.when(owner != me)
            def _():
                gap_copy(step, owner).wait_send()

            return 0

        lax.fori_loop(0, shards, drain, 0)


def solution(mesh):
    reps, shards = mesh.shape["rep"], mesh.shape["fsdp"]

    def local(
        latents, gaussian, stamps, numerator, momentum, push_weight, arrived, arrived_weight
    ):
        steps, samples, channels, pixels = latents.shape
        rows, columns = numerator.shape[1:]
        assert samples == 1 and steps == STEPS
        padded = -(-rows // 16) * 16
        chunk = 16 if rows % 16 == 0 else rows
        parts = rows // chunk
        vmem = pl.BlockSpec(memory_space=pltpu.VMEM)
        dma = pltpu.SemaphoreType.DMA
        state = jax.ShapeDtypeStruct((rows, columns), jnp.float32)
        one = jax.ShapeDtypeStruct((1, 1), jnp.float32)
        outs = pl.pallas_call(
            functools.partial(body, (reps, shards, padded, chunk)),
            out_shape=(state, state, one, state, one),
            in_specs=[pl.BlockSpec(memory_space=pltpu.SMEM)] + [vmem] * 7,
            out_specs=(vmem,) * 5,
            scratch_shapes=[
                pltpu.VMEM((steps, shards, channels, pixels), jnp.float32),
                pltpu.VMEM((steps, shards, rows, pixels), jnp.float32),
                pltpu.VMEM((steps, shards, rows, pixels), jnp.float32),
                pltpu.VMEM((TAPS * padded, channels), jnp.bfloat16),
                pltpu.VMEM((TAPS * padded, channels), jnp.bfloat16),
                pltpu.VMEM((TAPS * padded, pixels), jnp.bfloat16),
                pltpu.VMEM((TAPS * padded, pixels), jnp.bfloat16),
                pltpu.VMEM((TAPS * padded, channels), jnp.float32),
                pltpu.VMEM((TAPS * padded, pixels), jnp.float32),
                pltpu.VMEM((steps, rows, columns), jnp.float32),
                pltpu.VMEM((rows, columns), jnp.float32),
                pltpu.VMEM((2, steps, 8, 128), jnp.float32),
                dma((2, steps, shards)),
                dma((steps, shards)),
                dma((steps, shards)),
                dma((steps, shards)),
                dma((steps, parts)),
                dma((steps, parts)),
                dma((steps,)),
                dma((steps,)),
            ],
            compiler_params=pltpu.CompilerParams(
                collective_id=0, has_side_effects=True, vmem_limit_bytes=60000 * 1024
            ),
        )(
            stamps,
            latents.reshape(steps, channels, pixels),
            gaussian.reshape(steps, channels, pixels),
            numerator[0],
            momentum[0],
            push_weight.reshape(1, 1),
            arrived[0],
            arrived_weight.reshape(1, 1),
        )
        return (outs[0][None], outs[1][None], outs[2][0], outs[3][None], outs[4][0])

    in_specs = (
        P(None, ("rep", "fsdp"), None, None),
        P(None, ("rep", "fsdp"), None, None),
        P(None, ("rep", "fsdp")),
        P("rep", "fsdp", None),
        P("rep", "fsdp", None),
        P("rep"),
        P("rep", "fsdp", None),
        P("rep"),
    )
    out_specs = (
        P("rep", "fsdp", None),
        P("rep", "fsdp", None),
        P("rep"),
        P("rep", "fsdp", None),
        P("rep"),
    )
    return jax.shard_map(local, mesh=mesh, in_specs=in_specs, out_specs=out_specs, check_vma=False)
```

```python
import functools

import jax
import jax.numpy as jnp
from jax import lax
from jax.experimental import pallas as pl
from jax.experimental.pallas import tpu as pltpu
from jax.sharding import PartitionSpec as P

GROUPS = 32
CROP_H = 16
CROP_W = 16
STEPS = 2
TRAIN_T = 1000
TAPS = 9

norm_epsilon = 1e-05
momentum_decay = 0.9
step_size = 1.0
beta_first = 0.00085
beta_last = 0.012
MESH = pl.DeviceIdType.MESH


def split(value):
    high = value.astype(jnp.bfloat16)
    return high, (value - high.astype(jnp.float32)).astype(jnp.bfloat16)


def product(a, b, contract):
    dims = ((contract[0], contract[1]), ((), ()))
    dot = functools.partial(
        lax.dot_general, dimension_numbers=dims, preferred_element_type=jnp.float32
    )
    return dot(a[0], b[0]) + (dot(a[0], b[1]) + dot(a[1], b[0]))


def noise_level(stamp):
    rows = -(-TRAIN_T // 128)
    shape = (rows, 128)
    position = lax.broadcasted_iota(jnp.int32, shape, 0) * 128 + lax.broadcasted_iota(
        jnp.int32, shape, 1
    )
    fraction = position.astype(jnp.float32) / (TRAIN_T - 1)
    root_first = beta_first**0.5
    root_last = beta_last**0.5
    root = root_first + fraction * (root_last - root_first)
    factor = jnp.where(position <= stamp, 1.0 - root * root, jnp.float32(1.0))
    for shift in (64, 32, 16, 8, 4, 2, 1):
        factor = factor * pltpu.roll(factor, shift, 1)
    for shift in (4, 2, 1):
        factor = factor * pltpu.roll(factor, shift, 0)
    return factor


def group_mean(value, same_group, count):
    row = jnp.sum(value, axis=1, keepdims=True)
    row = jnp.broadcast_to(row, (row.shape[0], 128))
    first = row.astype(jnp.bfloat16)
    rest = row - first.astype(jnp.float32)
    second = rest.astype(jnp.bfloat16)
    third = (rest - second.astype(jnp.float32)).astype(jnp.bfloat16)
    dot = functools.partial(jnp.dot, preferred_element_type=jnp.float32)
    total = dot(same_group, first) + (dot(same_group, second) + dot(same_group, third))
    return total[:, 0:1] * (1.0 / count)


def tap_shift(tap):
    return (tap // 3 - 1) * CROP_W + (tap % 3 - 1)


def tap_mask(tap, pixels):
    place = lax.broadcasted_iota(jnp.int32, (1, pixels), 1)
    row = place // CROP_W + (tap // 3 - 1)
    col = place % CROP_W + (tap % 3 - 1)
    return (row >= 0) & (row < CROP_H) & (col >= 0) & (col < CROP_W)


def body(
    sizes,
    stamps, weight, arrived_weight,
    latents_in, gaussian_in, numerator_in, momentum_in, arrived_in,
    numerator_out, momentum_out, weight_out, pending_out, pending_weight_out,
    latents, gaussian, numerator, momentum, arrived, fetch_sem,
    acts, gap_own, gap_rows, kernel_hi, kernel_lo, res_hi, res_lo, total, taps_out,
    outbox, inbox, weight_box,
    acts_send, acts_recv, gap_send, gap_recv, push_send, push_recv, weight_send, weight_recv,
):
    reps, shards, padded, chunk = sizes
    rows, columns = numerator.shape
    channels, pixels = latents.shape[1:]
    replica_batch = shards
    tap_scale = columns ** (-0.5)
    rep = lax.axis_index("rep")
    me = lax.axis_index("fsdp")

    def fetch(index, source, target):
        return pltpu.make_async_copy(source, target, fetch_sem.at[index])

    samples_in = [
        (
            fetch(2 * step, latents_in.at[step], latents.at[step]),
            fetch(2 * step + 1, gaussian_in.at[step], gaussian.at[step]),
        )
        for step in range(STEPS)
    ]
    state_in = [
        fetch(2 * STEPS, numerator_in, numerator),
        fetch(2 * STEPS + 1, momentum_in, momentum),
        fetch(2 * STEPS + 2, arrived_in, arrived),
    ]
    for pair in samples_in:
        for copy in pair:
            copy.start()
    for copy in state_in:
        copy.start()

    offsets = sorted({2**k % reps for k in range(STEPS)} | {-(2**k) % reps for k in range(STEPS)})
    barrier = pltpu.get_barrier_semaphore()
    for offset in range(1, shards):
        pl.semaphore_signal(
            barrier, inc=1, device_id={"fsdp": lax.rem(me + offset, shards)}, device_id_type=MESH
        )
    for offset in offsets:
        pl.semaphore_signal(
            barrier, inc=1, device_id={"rep": lax.rem(rep + offset, reps)}, device_id_type=MESH
        )

    def acts_copy(step, owner, right):
        side = 1 if right else 0
        return pltpu.make_async_remote_copy(
            src_ref=acts.at[step, owner],
            dst_ref=acts.at[step, owner],
            send_sem=acts_send.at[side, step, owner],
            recv_sem=acts_recv.at[step, owner],
            device_id={"fsdp": me + 1 if right else me - 1},
            device_id_type=MESH,
        )

    def gap_copy(step, target):
        return pltpu.make_async_remote_copy(
            src_ref=gap_own.at[step, target],
            dst_ref=gap_rows.at[step, me],
            send_sem=gap_send.at[step, target],
            recv_sem=gap_recv.at[step, me],
            device_id={"fsdp": target},
            device_id_type=MESH,
        )

    def gap_arrival(step, owner):
        return pltpu.make_async_remote_copy(
            src_ref=gap_own.at[step, owner],
            dst_ref=gap_rows.at[step, owner],
            send_sem=gap_send.at[step, owner],
            recv_sem=gap_recv.at[step, owner],
            device_id={"fsdp": owner},
            device_id_type=MESH,
        )

    def push_copy(step, part):
        span = pl.ds(part * chunk, chunk)
        target = (inbox if step < STEPS - 1 else pending_out).at[span]
        return pltpu.make_async_remote_copy(
            src_ref=outbox.at[step, span],
            dst_ref=target,
            send_sem=push_send.at[step, part],
            recv_sem=push_recv.at[step, part],
            device_id={"rep": lax.rem(rep + 2**step, reps)},
            device_id_type=MESH,
        )

    def weight_copy(step):
        return pltpu.make_async_remote_copy(
            src_ref=weight_box.at[0, step],
            dst_ref=weight_box.at[1, step],
            send_sem=weight_send.at[step],
            recv_sem=weight_recv.at[step],
            device_id={"rep": lax.rem(rep + 2**step, reps)},
            device_id_type=MESH,
        )

    def send_own(step, right):
        @pl.when(me < shards - 1 if right else me > 0)
        def _():
            acts_copy(step, me, right).start()
            for away in range(1, shards):
                target = me + away if right else me - away

                @pl.when(target < shards if right else target >= 0)
                def _():
                    gap_copy(step, target).start()

    same_group = (
        lax.broadcasted_iota(jnp.int32, (channels, channels), 0) // (channels // GROUPS)
        == lax.broadcasted_iota(jnp.int32, (channels, channels), 1) // (channels // GROUPS)
    ).astype(jnp.float32).astype(jnp.bfloat16)
    count = (channels // GROUPS) * pixels

    def activate(step):
        level = noise_level(stamps[step])[0:1, 0:1]
        for copy in samples_in[step]:
            copy.wait()
        noise = gaussian[step]
        noised = jnp.sqrt(level) * latents[step] + jnp.sqrt(1.0 - level) * noise
        gap = noised - noise
        for target in range(shards):
            gap_own[step, target] = gap[target * rows : (target + 1) * rows]
        centered = noised - group_mean(noised, same_group, count)
        spread = group_mean(centered * centered, same_group, count)
        normed = centered * lax.rsqrt(spread + norm_epsilon)
        acts[step, me] = normed / (1.0 + jnp.exp(-normed))
        gap_rows[step, me] = gap_own[step, me]

    activate(0)
    first_weight = jnp.broadcast_to(weight[...], weight_box.shape[2:])
    weight_box[0, 0] = 0.5 * first_weight
    second_weight = 0.5 * first_weight + jnp.broadcast_to(
        arrived_weight[...], weight_box.shape[2:]
    )
    weight_box[0, 1] = 0.5 * second_weight
    pl.semaphore_wait(barrier, shards - 1 + len(offsets))
    send_own(0, True)
    send_own(0, False)
    for step in range(STEPS):
        weight_copy(step).start()
    for step in range(1, STEPS):
        activate(step)

    @pl.when(me == 0)
    def _():
        for step in range(1, STEPS):
            send_own(step, True)

    @pl.when(me == shards - 1)
    def _():
        for step in range(1, STEPS):
            send_own(step, False)

    if padded != rows:
        for ref in (kernel_hi, kernel_lo, res_hi, res_lo):
            ref[...] = jnp.zeros(ref.shape, ref.dtype)

    def set_kernel(tap, first, values):
        high, low = split(values)
        start = tap * padded + first
        kernel_hi[start : start + values.shape[0]] = high
        kernel_lo[start : start + values.shape[0]] = low

    for copy in state_in:
        copy.wait()
    for tap in range(TAPS):
        set_kernel(
            tap, 0, numerator[:, tap * channels : (tap + 1) * channels] / first_weight[0:1, 0:1]
        )

    def process(step, owner):
        signal = split(acts[step, owner])
        taps_out[...] = product((kernel_hi[...], kernel_lo[...]), signal, ((1,), (0,)))
        output = jnp.zeros((rows, pixels), jnp.float32)
        for tap in range(TAPS):
            value = taps_out[tap * padded : tap * padded + rows]
            moved = pltpu.roll(value, -tap_shift(tap) % pixels, 1) if tap_shift(tap) else value
            output += jnp.where(tap_mask(tap, pixels), moved, 0.0)
        residual = gap_rows[step, owner] + tap_scale * output
        for tap in range(TAPS):
            value = jnp.where(tap_mask(tap, pixels), residual, 0.0)
            if tap_shift(tap):
                value = pltpu.roll(value, tap_shift(tap) % pixels, 1)
            high, low = split(value)
            res_hi[tap * padded : tap * padded + rows] = high
            res_lo[tap * padded : tap * padded + rows] = low
        total[...] += product((res_hi[...], res_lo[...]), signal, ((1,), (1,)))

    for step in range(STEPS):
        total[...] = jnp.zeros(total.shape, jnp.float32)

        def visit(k, _, step=step):
            away = (k + 1) // 2
            owner = jnp.where(lax.rem(k, 2) == 1, me - away, me + away)

            @pl.when((owner >= 0) & (owner < shards))
            def _():
                @pl.when(owner < me)
                def _():
                    acts_copy(step, owner, True).wait_recv()

                    @pl.when(me < shards - 1)
                    def _():
                        acts_copy(step, owner, True).start()

                    if step < STEPS - 1:

                        @pl.when(owner == 0)
                        def _():
                            send_own(step + 1, True)

                @pl.when(owner > me)
                def _():
                    acts_copy(step, owner, False).wait_recv()

                    @pl.when(me > 0)
                    def _():
                        acts_copy(step, owner, False).start()

                    if step < STEPS - 1:

                        @pl.when(owner == shards - 1)
                        def _():
                            send_own(step + 1, False)

                @pl.when(owner != me)
                def _():
                    gap_arrival(step, owner).wait_recv()

                process(step, owner)

            return 0

        lax.fori_loop(0, 2 * shards - 1, visit, 0)

        if step > 0:
            for part in range(rows // chunk):
                push_copy(step - 1, part).wait_recv()
        for part in range(rows // chunk):
            span = slice(part * chunk, (part + 1) * chunk)
            for tap in range(TAPS):
                cut = slice(tap * channels, (tap + 1) * channels)
                start = tap * padded + part * chunk
                gradient = total[start : start + chunk] * (tap_scale / replica_batch)
                old = (momentum if step == 0 else momentum_out)[span, cut]
                new = momentum_decay * old + gradient
                momentum_out[span, cut] = new
                base = (numerator if step == 0 else numerator_out)[span, cut]
                half = 0.5 * (base - step_size * new)
                outbox[step, span, cut] = half
                fresh = half + (arrived if step == 0 else inbox)[span, cut]
                numerator_out[span, cut] = fresh
                if step < STEPS - 1:
                    set_kernel(tap, part * chunk, fresh / second_weight[0:1, 0:1])
            push_copy(step, part).start()

    for step in range(STEPS):
        weight_copy(step).wait_recv()
    weight_out[...] = (0.5 * second_weight + weight_box[1, 0])[0:1, 0:1]
    pending_weight_out[...] = weight_box[1, 1][0:1, 0:1]
    for step in range(STEPS):
        weight_copy(step).wait_send()
        for part in range(rows // chunk):
            push_copy(step, part).wait_send()
            if step == STEPS - 1:
                push_copy(step, part).wait_recv()

        def drain(owner, _, step=step):
            @pl.when((owner <= me) & (me < shards - 1))
            def _():
                acts_copy(step, owner, True).wait_send()

            @pl.when((owner >= me) & (me > 0))
            def _():
                acts_copy(step, owner, False).wait_send()

            @pl.when(owner != me)
            def _():
                gap_copy(step, owner).wait_send()

            return 0

        lax.fori_loop(0, shards, drain, 0)


def deliver(first_in, second_in, third_in, first_out, second_out, third_out, sems):
    pairs = ((first_in, first_out), (second_in, second_out), (third_in, third_out))
    copies = [
        pltpu.make_async_copy(source, target, sems.at[k])
        for k, (source, target) in enumerate(pairs)
    ]
    for copy in copies:
        copy.start()
    for copy in copies:
        copy.wait()


def solution(mesh):
    reps, shards = mesh.shape["rep"], mesh.shape["fsdp"]

    def local(
        latents, gaussian, stamps, numerator, momentum, push_weight, arrived, arrived_weight
    ):
        steps, samples, channels, pixels = latents.shape
        rows, columns = numerator.shape[1:]
        assert samples == 1 and steps == STEPS
        padded = -(-rows // 16) * 16
        chunk = 16 if rows % 16 == 0 else rows
        parts = rows // chunk
        vmem = pl.BlockSpec(memory_space=pltpu.VMEM)
        dma = pltpu.SemaphoreType.DMA
        state = pltpu.VMEM((rows, columns), jnp.float32)
        one = jax.ShapeDtypeStruct((1, 1), jnp.float32)
        outs = pl.pallas_call(
            functools.partial(body, (reps, shards, padded, chunk)),
            out_shape=(state, state, one, state, one),
            in_specs=[pl.BlockSpec(memory_space=pltpu.SMEM), vmem, vmem]
            + [pl.BlockSpec(memory_space=pl.ANY)] * 5,
            out_specs=(vmem,) * 5,
            scratch_shapes=[
                pltpu.VMEM((steps, channels, pixels), jnp.float32),
                pltpu.VMEM((steps, channels, pixels), jnp.float32),
                pltpu.VMEM((rows, columns), jnp.float32),
                pltpu.VMEM((rows, columns), jnp.float32),
                pltpu.VMEM((rows, columns), jnp.float32),
                dma((2 * steps + 3,)),
                pltpu.VMEM((steps, shards, channels, pixels), jnp.float32),
                pltpu.VMEM((steps, shards, rows, pixels), jnp.float32),
                pltpu.VMEM((steps, shards, rows, pixels), jnp.float32),
                pltpu.VMEM((TAPS * padded, channels), jnp.bfloat16),
                pltpu.VMEM((TAPS * padded, channels), jnp.bfloat16),
                pltpu.VMEM((TAPS * padded, pixels), jnp.bfloat16),
                pltpu.VMEM((TAPS * padded, pixels), jnp.bfloat16),
                pltpu.VMEM((TAPS * padded, channels), jnp.float32),
                pltpu.VMEM((TAPS * padded, pixels), jnp.float32),
                pltpu.VMEM((steps, rows, columns), jnp.float32),
                pltpu.VMEM((rows, columns), jnp.float32),
                pltpu.VMEM((2, steps, 8, 128), jnp.float32),
                dma((2, steps, shards)),
                dma((steps, shards)),
                dma((steps, shards)),
                dma((steps, shards)),
                dma((steps, parts)),
                dma((steps, parts)),
                dma((steps,)),
                dma((steps,)),
            ],
            compiler_params=pltpu.CompilerParams(
                collective_id=0, has_side_effects=True, vmem_limit_bytes=56 * 1024 * 1024
            ),
        )(
            stamps.reshape(steps),
            push_weight.reshape(1, 1),
            arrived_weight.reshape(1, 1),
            latents.reshape(steps, channels, pixels),
            gaussian.reshape(steps, channels, pixels),
            numerator[0],
            momentum[0],
            arrived[0],
        )
        stored = jax.ShapeDtypeStruct((rows, columns), jnp.float32)
        results = pl.pallas_call(
            deliver,
            out_shape=(stored,) * 3,
            in_specs=[vmem] * 3,
            out_specs=(pl.BlockSpec(memory_space=pl.ANY),) * 3,
            scratch_shapes=[dma((3,))],
            compiler_params=pltpu.CompilerParams(vmem_limit_bytes=48 * 1024 * 1024),
        )(outs[0], outs[1], outs[3])
        return (results[0][None], results[1][None], outs[2][0], results[2][None], outs[4][0])

    in_specs = (
        P(None, ("rep", "fsdp"), None, None),
        P(None, ("rep", "fsdp"), None, None),
        P(None, ("rep", "fsdp")),
        P("rep", "fsdp", None),
        P("rep", "fsdp", None),
        P("rep"),
        P("rep", "fsdp", None),
        P("rep"),
    )
    out_specs = (
        P("rep", "fsdp", None),
        P("rep", "fsdp", None),
        P("rep"),
        P("rep", "fsdp", None),
        P("rep"),
    )
    return jax.shard_map(local, mesh=mesh, in_specs=in_specs, out_specs=out_specs, check_vma=False)
```

```python
import functools

import jax
import jax.numpy as jnp
from jax import lax
from jax.experimental import pallas as pl
from jax.experimental.pallas import tpu as pltpu
from jax.sharding import PartitionSpec as P

GROUPS = 32
CROP_H = 16
CROP_W = 16
STEPS = 2
TRAIN_T = 1000
TAPS = 9

norm_epsilon = 1e-05
momentum_decay = 0.9
step_size = 1.0
beta_first = 0.00085
beta_last = 0.012
MESH = pl.DeviceIdType.MESH


def split(value):
    high = value.astype(jnp.bfloat16)
    return high, (value - high.astype(jnp.float32)).astype(jnp.bfloat16)


def product(a, b, contract):
    dims = ((contract[0], contract[1]), ((), ()))
    dot = functools.partial(
        lax.dot_general, dimension_numbers=dims, preferred_element_type=jnp.float32
    )
    return dot(a[0], b[0]) + (dot(a[0], b[1]) + dot(a[1], b[0]))


def noise_level(stamp):
    rows = -(-TRAIN_T // 128)
    shape = (rows, 128)
    position = lax.broadcasted_iota(jnp.int32, shape, 0) * 128 + lax.broadcasted_iota(
        jnp.int32, shape, 1
    )
    fraction = position.astype(jnp.float32) / (TRAIN_T - 1)
    root_first = beta_first**0.5
    root_last = beta_last**0.5
    root = root_first + fraction * (root_last - root_first)
    factor = jnp.where(position <= stamp, 1.0 - root * root, jnp.float32(1.0))
    for shift in (64, 32, 16, 8, 4, 2, 1):
        factor = factor * pltpu.roll(factor, shift, 1)
    for shift in (4, 2, 1):
        factor = factor * pltpu.roll(factor, shift, 0)
    return factor


def group_mean(value, same_group, count):
    row = jnp.sum(value, axis=1, keepdims=True)
    row = jnp.broadcast_to(row, (row.shape[0], 128))
    first = row.astype(jnp.bfloat16)
    rest = row - first.astype(jnp.float32)
    second = rest.astype(jnp.bfloat16)
    third = (rest - second.astype(jnp.float32)).astype(jnp.bfloat16)
    dot = functools.partial(jnp.dot, preferred_element_type=jnp.float32)
    total = dot(same_group, first) + (dot(same_group, second) + dot(same_group, third))
    return total[:, 0:1] * (1.0 / count)


def tap_shift(tap):
    return (tap // 3 - 1) * CROP_W + (tap % 3 - 1)


def tap_mask(tap, pixels):
    place = lax.broadcasted_iota(jnp.int32, (1, pixels), 1)
    row = place // CROP_W + (tap // 3 - 1)
    col = place % CROP_W + (tap % 3 - 1)
    return (row >= 0) & (row < CROP_H) & (col >= 0) & (col < CROP_W)


def body(
    sizes,
    stamps, weight, arrived_weight,
    latents_in, gaussian_in, numerator_in, momentum_in, arrived_in,
    numerator_out, momentum_out, weight_out, pending_out, pending_weight_out,
    latents, gaussian, numerator, momentum, arrived, fetch_sem,
    acts, gap_own, gap_rows, kernel_hi, kernel_lo, res_hi, res_lo, total, taps_out,
    outbox, inbox, weight_box, relay_box, relay_sem,
    acts_send, acts_recv, gap_send, gap_recv, push_send, push_recv, weight_send, weight_recv,
):
    reps, shards, padded, chunk = sizes
    rows, columns = numerator.shape
    channels, pixels = latents.shape[1:]
    replica_batch = shards
    tap_scale = columns ** (-0.5)
    rep = lax.axis_index("rep")
    me = lax.axis_index("fsdp")

    def fetch(index, source, target):
        return pltpu.make_async_copy(source, target, fetch_sem.at[index])

    samples_in = [
        (
            fetch(2 * step, latents_in.at[step], latents.at[step]),
            fetch(2 * step + 1, gaussian_in.at[step], gaussian.at[step]),
        )
        for step in range(STEPS)
    ]
    state_in = [
        fetch(2 * STEPS, numerator_in, numerator),
        fetch(2 * STEPS + 1, momentum_in, momentum),
        fetch(2 * STEPS + 2, arrived_in, arrived),
    ]
    for pair in samples_in:
        for copy in pair:
            copy.start()
    for copy in state_in:
        copy.start()

    offsets = sorted({2**k % reps for k in range(STEPS)} | {-(2**k) % reps for k in range(STEPS)})
    barrier = pltpu.get_barrier_semaphore()
    for offset in range(1, shards):
        pl.semaphore_signal(
            barrier, inc=1, device_id={"fsdp": lax.rem(me + offset, shards)}, device_id_type=MESH
        )
    for offset in offsets:
        pl.semaphore_signal(
            barrier, inc=1, device_id={"rep": lax.rem(rep + offset, reps)}, device_id_type=MESH
        )

    detour = shards >= 4
    last_part = rows // chunk - 1
    at_end = (me == 0) | (me == shards - 1)
    beside_end = (me == 1) | (me == shards - 2)
    end = jnp.where(me <= 1, 0, shards - 1)
    beside = jnp.where(me <= 1, 1, shards - 2)
    last_shift = 2 ** (STEPS - 1)
    if detour:

        @pl.when(at_end)
        def _():
            pl.semaphore_signal(
                barrier,
                inc=1,
                device_id={"rep": lax.rem(rep + last_shift, reps), "fsdp": beside},
                device_id_type=MESH,
            )

        @pl.when(beside_end)
        def _():
            pl.semaphore_signal(
                barrier,
                inc=1,
                device_id={"rep": lax.rem(rep + reps - last_shift % reps, reps), "fsdp": end},
                device_id_type=MESH,
            )

    def to_relay():
        return pltpu.make_async_remote_copy(
            src_ref=outbox.at[STEPS - 1, pl.ds(last_part * chunk, chunk)],
            dst_ref=relay_box,
            send_sem=relay_sem.at[0],
            recv_sem=relay_sem.at[1],
            device_id={"rep": lax.rem(rep + last_shift, reps), "fsdp": beside},
            device_id_type=MESH,
        )

    def from_relay():
        return pltpu.make_async_remote_copy(
            src_ref=relay_box,
            dst_ref=pending_out.at[pl.ds(last_part * chunk, chunk)],
            send_sem=relay_sem.at[2],
            recv_sem=push_recv.at[STEPS - 1, last_part],
            device_id={"fsdp": end},
            device_id_type=MESH,
        )

    def acts_copy(step, owner, right):
        side = 1 if right else 0
        return pltpu.make_async_remote_copy(
            src_ref=acts.at[step, owner],
            dst_ref=acts.at[step, owner],
            send_sem=acts_send.at[side, step, owner],
            recv_sem=acts_recv.at[step, owner],
            device_id={"fsdp": me + 1 if right else me - 1},
            device_id_type=MESH,
        )

    def gap_copy(step, target):
        return pltpu.make_async_remote_copy(
            src_ref=gap_own.at[step, target],
            dst_ref=gap_rows.at[step, me],
            send_sem=gap_send.at[step, target],
            recv_sem=gap_recv.at[step, me],
            device_id={"fsdp": target},
            device_id_type=MESH,
        )

    def gap_arrival(step, owner):
        return pltpu.make_async_remote_copy(
            src_ref=gap_own.at[step, owner],
            dst_ref=gap_rows.at[step, owner],
            send_sem=gap_send.at[step, owner],
            recv_sem=gap_recv.at[step, owner],
            device_id={"fsdp": owner},
            device_id_type=MESH,
        )

    def push_copy(step, part):
        span = pl.ds(part * chunk, chunk)
        target = (inbox if step < STEPS - 1 else pending_out).at[span]
        return pltpu.make_async_remote_copy(
            src_ref=outbox.at[step, span],
            dst_ref=target,
            send_sem=push_send.at[step, part],
            recv_sem=push_recv.at[step, part],
            device_id={"rep": lax.rem(rep + 2**step, reps)},
            device_id_type=MESH,
        )

    def weight_copy(step):
        return pltpu.make_async_remote_copy(
            src_ref=weight_box.at[0, step],
            dst_ref=weight_box.at[1, step],
            send_sem=weight_send.at[step],
            recv_sem=weight_recv.at[step],
            device_id={"rep": lax.rem(rep + 2**step, reps)},
            device_id_type=MESH,
        )

    def send_own(step, right):
        @pl.when(me < shards - 1 if right else me > 0)
        def _():
            acts_copy(step, me, right).start()
            for away in range(1, shards):
                target = me + away if right else me - away

                @pl.when(target < shards if right else target >= 0)
                def _():
                    gap_copy(step, target).start()

    same_group = (
        lax.broadcasted_iota(jnp.int32, (channels, channels), 0) // (channels // GROUPS)
        == lax.broadcasted_iota(jnp.int32, (channels, channels), 1) // (channels // GROUPS)
    ).astype(jnp.float32).astype(jnp.bfloat16)
    count = (channels // GROUPS) * pixels

    def activate(step):
        level = noise_level(stamps[step])[0:1, 0:1]
        for copy in samples_in[step]:
            copy.wait()
        noise = gaussian[step]
        noised = jnp.sqrt(level) * latents[step] + jnp.sqrt(1.0 - level) * noise
        gap = noised - noise
        for target in range(shards):
            gap_own[step, target] = gap[target * rows : (target + 1) * rows]
        centered = noised - group_mean(noised, same_group, count)
        spread = group_mean(centered * centered, same_group, count)
        normed = centered * lax.rsqrt(spread + norm_epsilon)
        acts[step, me] = normed / (1.0 + jnp.exp(-normed))
        gap_rows[step, me] = gap_own[step, me]

    activate(0)
    first_weight = jnp.broadcast_to(weight[...], weight_box.shape[2:])
    weight_box[0, 0] = 0.5 * first_weight
    second_weight = 0.5 * first_weight + jnp.broadcast_to(
        arrived_weight[...], weight_box.shape[2:]
    )
    weight_box[0, 1] = 0.5 * second_weight
    peers = shards - 1 + len(offsets)
    if detour:
        peers = peers + jnp.where(at_end | beside_end, 1, 0)
    pl.semaphore_wait(barrier, peers)
    send_own(0, True)
    send_own(0, False)
    for step in range(STEPS):
        weight_copy(step).start()
    for step in range(1, STEPS):
        activate(step)

    @pl.when(me == 0)
    def _():
        for step in range(1, STEPS):
            send_own(step, True)

    @pl.when(me == shards - 1)
    def _():
        for step in range(1, STEPS):
            send_own(step, False)

    if padded != rows:
        for ref in (kernel_hi, kernel_lo, res_hi, res_lo):
            ref[...] = jnp.zeros(ref.shape, ref.dtype)

    def set_kernel(tap, first, values):
        high, low = split(values)
        start = tap * padded + first
        kernel_hi[start : start + values.shape[0]] = high
        kernel_lo[start : start + values.shape[0]] = low

    for copy in state_in:
        copy.wait()
    for tap in range(TAPS):
        set_kernel(
            tap, 0, numerator[:, tap * channels : (tap + 1) * channels] / first_weight[0:1, 0:1]
        )

    def process(step, owner):
        signal = split(acts[step, owner])
        taps_out[...] = product((kernel_hi[...], kernel_lo[...]), signal, ((1,), (0,)))
        output = jnp.zeros((rows, pixels), jnp.float32)
        for tap in range(TAPS):
            value = taps_out[tap * padded : tap * padded + rows]
            moved = pltpu.roll(value, -tap_shift(tap) % pixels, 1) if tap_shift(tap) else value
            output += jnp.where(tap_mask(tap, pixels), moved, 0.0)
        residual = gap_rows[step, owner] + tap_scale * output
        for tap in range(TAPS):
            value = jnp.where(tap_mask(tap, pixels), residual, 0.0)
            if tap_shift(tap):
                value = pltpu.roll(value, tap_shift(tap) % pixels, 1)
            high, low = split(value)
            res_hi[tap * padded : tap * padded + rows] = high
            res_lo[tap * padded : tap * padded + rows] = low
        total[...] += product((res_hi[...], res_lo[...]), signal, ((1,), (1,)))

    for step in range(STEPS):
        total[...] = jnp.zeros(total.shape, jnp.float32)

        def visit(k, _, step=step):
            away = (k + 1) // 2
            owner = jnp.where(lax.rem(k, 2) == 1, me - away, me + away)

            @pl.when((owner >= 0) & (owner < shards))
            def _():
                @pl.when(owner < me)
                def _():
                    acts_copy(step, owner, True).wait_recv()

                    @pl.when(me < shards - 1)
                    def _():
                        acts_copy(step, owner, True).start()

                    if step < STEPS - 1:

                        @pl.when(owner == 0)
                        def _():
                            send_own(step + 1, True)

                @pl.when(owner > me)
                def _():
                    acts_copy(step, owner, False).wait_recv()

                    @pl.when(me > 0)
                    def _():
                        acts_copy(step, owner, False).start()

                    if step < STEPS - 1:

                        @pl.when(owner == shards - 1)
                        def _():
                            send_own(step + 1, False)

                @pl.when(owner != me)
                def _():
                    gap_arrival(step, owner).wait_recv()

                process(step, owner)

            return 0

        lax.fori_loop(0, 2 * shards - 1, visit, 0)

        if step > 0:
            for part in range(rows // chunk):
                push_copy(step - 1, part).wait_recv()
        order = list(range(rows // chunk))
        for part in order[-1:] + order[:-1]:
            span = slice(part * chunk, (part + 1) * chunk)
            for tap in range(TAPS):
                cut = slice(tap * channels, (tap + 1) * channels)
                start = tap * padded + part * chunk
                gradient = total[start : start + chunk] * (tap_scale / replica_batch)
                old = (momentum if step == 0 else momentum_out)[span, cut]
                new = momentum_decay * old + gradient
                momentum_out[span, cut] = new
                base = (numerator if step == 0 else numerator_out)[span, cut]
                half = 0.5 * (base - step_size * new)
                outbox[step, span, cut] = half
                fresh = half + (arrived if step == 0 else inbox)[span, cut]
                numerator_out[span, cut] = fresh
                if step < STEPS - 1:
                    set_kernel(tap, part * chunk, fresh / second_weight[0:1, 0:1])
            if detour and step == STEPS - 1 and part == last_part:

                @pl.when(at_end)
                def _():
                    to_relay().start()

                @pl.when(jnp.logical_not(at_end))
                def _():
                    push_copy(STEPS - 1, last_part).start()

            else:
                push_copy(step, part).start()

    if detour:

        @pl.when(beside_end)
        def _():
            to_relay().wait_recv()
            from_relay().start()

    for step in range(STEPS):
        weight_copy(step).wait_recv()
    weight_out[...] = (0.5 * second_weight + weight_box[1, 0])[0:1, 0:1]
    pending_weight_out[...] = weight_box[1, 1][0:1, 0:1]
    for step in range(STEPS):
        weight_copy(step).wait_send()
        for part in range(rows // chunk):
            if detour and step == STEPS - 1 and part == last_part:

                @pl.when(at_end)
                def _():
                    to_relay().wait_send()

                @pl.when(jnp.logical_not(at_end))
                def _():
                    push_copy(STEPS - 1, last_part).wait_send()

                @pl.when(beside_end)
                def _():
                    from_relay().wait_send()

            else:
                push_copy(step, part).wait_send()
            if step == STEPS - 1:
                push_copy(step, part).wait_recv()

        def drain(owner, _, step=step):
            @pl.when((owner <= me) & (me < shards - 1))
            def _():
                acts_copy(step, owner, True).wait_send()

            @pl.when((owner >= me) & (me > 0))
            def _():
                acts_copy(step, owner, False).wait_send()

            @pl.when(owner != me)
            def _():
                gap_copy(step, owner).wait_send()

            return 0

        lax.fori_loop(0, shards, drain, 0)


def deliver(first_in, second_in, third_in, first_out, second_out, third_out, sems):
    pairs = ((first_in, first_out), (second_in, second_out), (third_in, third_out))
    copies = [
        pltpu.make_async_copy(source, target, sems.at[k])
        for k, (source, target) in enumerate(pairs)
    ]
    for copy in copies:
        copy.start()
    for copy in copies:
        copy.wait()


def solution(mesh):
    reps, shards = mesh.shape["rep"], mesh.shape["fsdp"]

    def local(
        latents, gaussian, stamps, numerator, momentum, push_weight, arrived, arrived_weight
    ):
        steps, samples, channels, pixels = latents.shape
        rows, columns = numerator.shape[1:]
        assert samples == 1 and steps == STEPS
        padded = -(-rows // 16) * 16
        chunk = 16 if rows % 16 == 0 else rows
        parts = rows // chunk
        vmem = pl.BlockSpec(memory_space=pltpu.VMEM)
        dma = pltpu.SemaphoreType.DMA
        state = pltpu.VMEM((rows, columns), jnp.float32)
        one = jax.ShapeDtypeStruct((1, 1), jnp.float32)
        outs = pl.pallas_call(
            functools.partial(body, (reps, shards, padded, chunk)),
            out_shape=(state, state, one, state, one),
            in_specs=[pl.BlockSpec(memory_space=pltpu.SMEM), vmem, vmem]
            + [pl.BlockSpec(memory_space=pl.ANY)] * 5,
            out_specs=(vmem,) * 5,
            scratch_shapes=[
                pltpu.VMEM((steps, channels, pixels), jnp.float32),
                pltpu.VMEM((steps, channels, pixels), jnp.float32),
                pltpu.VMEM((rows, columns), jnp.float32),
                pltpu.VMEM((rows, columns), jnp.float32),
                pltpu.VMEM((rows, columns), jnp.float32),
                dma((2 * steps + 3,)),
                pltpu.VMEM((steps, shards, channels, pixels), jnp.float32),
                pltpu.VMEM((steps, shards, rows, pixels), jnp.float32),
                pltpu.VMEM((steps, shards, rows, pixels), jnp.float32),
                pltpu.VMEM((TAPS * padded, channels), jnp.bfloat16),
                pltpu.VMEM((TAPS * padded, channels), jnp.bfloat16),
                pltpu.VMEM((TAPS * padded, pixels), jnp.bfloat16),
                pltpu.VMEM((TAPS * padded, pixels), jnp.bfloat16),
                pltpu.VMEM((TAPS * padded, channels), jnp.float32),
                pltpu.VMEM((TAPS * padded, pixels), jnp.float32),
                pltpu.VMEM((steps, rows, columns), jnp.float32),
                pltpu.VMEM((rows, columns), jnp.float32),
                pltpu.VMEM((2, steps, 8, 128), jnp.float32),
                pltpu.VMEM((chunk, columns), jnp.float32),
                dma((3,)),
                dma((2, steps, shards)),
                dma((steps, shards)),
                dma((steps, shards)),
                dma((steps, shards)),
                dma((steps, parts)),
                dma((steps, parts)),
                dma((steps,)),
                dma((steps,)),
            ],
            compiler_params=pltpu.CompilerParams(
                collective_id=0, has_side_effects=True, vmem_limit_bytes=56 * 1024 * 1024
            ),
        )(
            stamps.reshape(steps),
            push_weight.reshape(1, 1),
            arrived_weight.reshape(1, 1),
            latents.reshape(steps, channels, pixels),
            gaussian.reshape(steps, channels, pixels),
            numerator[0],
            momentum[0],
            arrived[0],
        )
        stored = jax.ShapeDtypeStruct((rows, columns), jnp.float32)
        results = pl.pallas_call(
            deliver,
            out_shape=(stored,) * 3,
            in_specs=[vmem] * 3,
            out_specs=(pl.BlockSpec(memory_space=pl.ANY),) * 3,
            scratch_shapes=[dma((3,))],
            compiler_params=pltpu.CompilerParams(vmem_limit_bytes=48 * 1024 * 1024),
        )(outs[0], outs[1], outs[3])
        return (results[0][None], results[1][None], outs[2][0], results[2][None], outs[4][0])

    in_specs = (
        P(None, ("rep", "fsdp"), None, None),
        P(None, ("rep", "fsdp"), None, None),
        P(None, ("rep", "fsdp")),
        P("rep", "fsdp", None),
        P("rep", "fsdp", None),
        P("rep"),
        P("rep", "fsdp", None),
        P("rep"),
    )
    out_specs = (
        P("rep", "fsdp", None),
        P("rep", "fsdp", None),
        P("rep"),
        P("rep", "fsdp", None),
        P("rep"),
    )
    return jax.shard_map(local, mesh=mesh, in_specs=in_specs, out_specs=out_specs, check_vma=False)
```

```python
import functools

import jax
import jax.numpy as jnp
from jax import lax
from jax.experimental import pallas as pl
from jax.experimental.pallas import tpu as pltpu
from jax.sharding import PartitionSpec as P

GROUPS = 32
CROP_H = 16
CROP_W = 16
STEPS = 2
TRAIN_T = 1000
TAPS = 9

norm_epsilon = 1e-05
momentum_decay = 0.9
step_size = 1.0
beta_first = 0.00085
beta_last = 0.012
MESH = pl.DeviceIdType.MESH


def split(value):
    high = value.astype(jnp.bfloat16)
    return high, (value - high.astype(jnp.float32)).astype(jnp.bfloat16)


def product(a, b, contract):
    dims = ((contract[0], contract[1]), ((), ()))
    dot = functools.partial(
        lax.dot_general, dimension_numbers=dims, preferred_element_type=jnp.float32
    )
    return dot(a[0], b[0]) + (dot(a[0], b[1]) + dot(a[1], b[0]))


def noise_level(stamp):
    rows = -(-TRAIN_T // 128)
    shape = (rows, 128)
    position = lax.broadcasted_iota(jnp.int32, shape, 0) * 128 + lax.broadcasted_iota(
        jnp.int32, shape, 1
    )
    fraction = position.astype(jnp.float32) / (TRAIN_T - 1)
    root_first = beta_first**0.5
    root_last = beta_last**0.5
    root = root_first + fraction * (root_last - root_first)
    factor = jnp.where(position <= stamp, 1.0 - root * root, jnp.float32(1.0))
    for shift in (64, 32, 16, 8, 4, 2, 1):
        factor = factor * pltpu.roll(factor, shift, 1)
    for shift in (4, 2, 1):
        factor = factor * pltpu.roll(factor, shift, 0)
    return factor


def group_mean(value, same_group, count):
    row = jnp.sum(value, axis=1, keepdims=True)
    row = jnp.broadcast_to(row, (row.shape[0], 128))
    first = row.astype(jnp.bfloat16)
    rest = row - first.astype(jnp.float32)
    second = rest.astype(jnp.bfloat16)
    third = (rest - second.astype(jnp.float32)).astype(jnp.bfloat16)
    dot = functools.partial(jnp.dot, preferred_element_type=jnp.float32)
    total = dot(same_group, first) + (dot(same_group, second) + dot(same_group, third))
    return total[:, 0:1] * (1.0 / count)


def tap_shift(tap):
    return (tap // 3 - 1) * CROP_W + (tap % 3 - 1)


def tap_mask(tap, pixels):
    place = lax.broadcasted_iota(jnp.int32, (1, pixels), 1)
    row = place // CROP_W + (tap // 3 - 1)
    col = place % CROP_W + (tap % 3 - 1)
    return (row >= 0) & (row < CROP_H) & (col >= 0) & (col < CROP_W)


def body(
    sizes,
    stamps, weight, arrived_weight,
    latents_in, gaussian_in, numerator_in, momentum_in, arrived_in,
    numerator_out, momentum_out, weight_out, pending_out, pending_weight_out,
    latents, gaussian, numerator, momentum, arrived, fetch_sem,
    acts, gap_own, gap_rows, kernel_hi, kernel_lo, res_hi, res_lo, total, taps_out,
    outbox, inbox, weight_box, relay_box, relay_sem,
    acts_send, acts_recv, gap_send, gap_recv, push_send, push_recv, weight_send, weight_recv,
):
    reps, shards, padded, chunk = sizes
    rows, columns = numerator.shape
    channels, pixels = latents.shape[1:]
    replica_batch = shards
    tap_scale = columns ** (-0.5)
    rep = lax.axis_index("rep")
    me = lax.axis_index("fsdp")

    def fetch(index, source, target):
        return pltpu.make_async_copy(source, target, fetch_sem.at[index])

    samples_in = [
        (
            fetch(2 * step, latents_in.at[step], latents.at[step]),
            fetch(2 * step + 1, gaussian_in.at[step], gaussian.at[step]),
        )
        for step in range(STEPS)
    ]
    state_in = [
        fetch(2 * STEPS, numerator_in, numerator),
        fetch(2 * STEPS + 1, momentum_in, momentum),
        fetch(2 * STEPS + 2, arrived_in, arrived),
    ]
    for pair in samples_in:
        for copy in pair:
            copy.start()
    for copy in state_in:
        copy.start()

    offsets = sorted({2**k % reps for k in range(STEPS)} | {-(2**k) % reps for k in range(STEPS)})
    barrier = pltpu.get_barrier_semaphore()
    for offset in range(1, shards):
        pl.semaphore_signal(
            barrier, inc=1, device_id={"fsdp": lax.rem(me + offset, shards)}, device_id_type=MESH
        )
    for offset in offsets:
        pl.semaphore_signal(
            barrier, inc=1, device_id={"rep": lax.rem(rep + offset, reps)}, device_id_type=MESH
        )

    detour = shards >= 4
    last_part = rows // chunk - 1
    at_end = (me == 0) | (me == shards - 1)
    beside_end = (me == 1) | (me == shards - 2)
    end = jnp.where(me <= 1, 0, shards - 1)
    beside = jnp.where(me <= 1, 1, shards - 2)
    last_shift = 2 ** (STEPS - 1)
    if detour:

        @pl.when(at_end)
        def _():
            pl.semaphore_signal(
                barrier,
                inc=1,
                device_id={"rep": lax.rem(rep + last_shift, reps), "fsdp": beside},
                device_id_type=MESH,
            )

        @pl.when(beside_end)
        def _():
            pl.semaphore_signal(
                barrier,
                inc=1,
                device_id={"rep": lax.rem(rep + reps - last_shift % reps, reps), "fsdp": end},
                device_id_type=MESH,
            )

    def to_relay():
        return pltpu.make_async_remote_copy(
            src_ref=outbox.at[STEPS - 1, pl.ds(last_part * chunk, chunk)],
            dst_ref=relay_box,
            send_sem=relay_sem.at[0],
            recv_sem=relay_sem.at[1],
            device_id={"rep": lax.rem(rep + last_shift, reps), "fsdp": beside},
            device_id_type=MESH,
        )

    def from_relay():
        return pltpu.make_async_remote_copy(
            src_ref=relay_box,
            dst_ref=pending_out.at[pl.ds(last_part * chunk, chunk)],
            send_sem=relay_sem.at[2],
            recv_sem=push_recv.at[STEPS - 1, last_part],
            device_id={"fsdp": end},
            device_id_type=MESH,
        )

    def acts_copy(step, owner, right):
        side = 1 if right else 0
        return pltpu.make_async_remote_copy(
            src_ref=acts.at[step, owner],
            dst_ref=acts.at[step, owner],
            send_sem=acts_send.at[side, step, owner],
            recv_sem=acts_recv.at[step, owner],
            device_id={"fsdp": me + 1 if right else me - 1},
            device_id_type=MESH,
        )

    def gap_copy(step, target):
        return pltpu.make_async_remote_copy(
            src_ref=gap_own.at[step, target],
            dst_ref=gap_rows.at[step, me],
            send_sem=gap_send.at[step, target],
            recv_sem=gap_recv.at[step, me],
            device_id={"fsdp": target},
            device_id_type=MESH,
        )

    def gap_arrival(step, owner):
        return pltpu.make_async_remote_copy(
            src_ref=gap_own.at[step, owner],
            dst_ref=gap_rows.at[step, owner],
            send_sem=gap_send.at[step, owner],
            recv_sem=gap_recv.at[step, owner],
            device_id={"fsdp": owner},
            device_id_type=MESH,
        )

    def push_copy(step, part):
        span = pl.ds(part * chunk, chunk)
        target = (inbox if step < STEPS - 1 else pending_out).at[span]
        return pltpu.make_async_remote_copy(
            src_ref=outbox.at[step, span],
            dst_ref=target,
            send_sem=push_send.at[step, part],
            recv_sem=push_recv.at[step, part],
            device_id={"rep": lax.rem(rep + 2**step, reps)},
            device_id_type=MESH,
        )

    def weight_copy(step):
        return pltpu.make_async_remote_copy(
            src_ref=weight_box.at[0, step],
            dst_ref=weight_box.at[1, step],
            send_sem=weight_send.at[step],
            recv_sem=weight_recv.at[step],
            device_id={"rep": lax.rem(rep + 2**step, reps)},
            device_id_type=MESH,
        )

    def send_own(step, right):
        @pl.when(me < shards - 1 if right else me > 0)
        def _():
            acts_copy(step, me, right).start()
            for away in range(1, shards):
                target = me + away if right else me - away

                @pl.when(target < shards if right else target >= 0)
                def _():
                    gap_copy(step, target).start()

    same_group = (
        lax.broadcasted_iota(jnp.int32, (channels, 1), 0) // (channels // GROUPS)
        == lax.broadcasted_iota(jnp.int32, (1, channels), 1) // (channels // GROUPS)
    ).astype(jnp.float32).astype(jnp.bfloat16)
    count = (channels // GROUPS) * pixels

    def activate(step):
        level = noise_level(stamps[step])[0:1, 0:1]
        for copy in samples_in[step]:
            copy.wait()
        noise = gaussian[step]
        noised = jnp.sqrt(level) * latents[step] + jnp.sqrt(1.0 - level) * noise
        gap = noised - noise
        for target in range(shards):
            gap_own[step, target] = gap[target * rows : (target + 1) * rows]
        centered = noised - group_mean(noised, same_group, count)
        spread = group_mean(centered * centered, same_group, count)
        normed = centered * lax.rsqrt(spread + norm_epsilon)
        acts[step, me] = normed / (1.0 + jnp.exp(-normed))
        gap_rows[step, me] = gap_own[step, me]

    activate(0)
    first_weight = jnp.broadcast_to(weight[...], weight_box.shape[2:])
    weight_box[0, 0] = 0.5 * first_weight
    second_weight = 0.5 * first_weight + jnp.broadcast_to(
        arrived_weight[...], weight_box.shape[2:]
    )
    weight_box[0, 1] = 0.5 * second_weight
    peers = shards - 1 + len(offsets)
    if detour:
        peers = peers + jnp.where(at_end | beside_end, 1, 0)
    pl.semaphore_wait(barrier, peers)
    send_own(0, True)
    send_own(0, False)
    for step in range(STEPS):
        weight_copy(step).start()
    for step in range(1, STEPS):
        activate(step)

    @pl.when(me == 0)
    def _():
        for step in range(1, STEPS):
            send_own(step, True)

    @pl.when(me == shards - 1)
    def _():
        for step in range(1, STEPS):
            send_own(step, False)

    if padded != rows:
        for ref in (kernel_hi, kernel_lo, res_hi, res_lo):
            ref[...] = jnp.zeros(ref.shape, ref.dtype)

    def set_kernel(tap, first, values):
        high, low = split(values)
        start = tap * padded + first
        kernel_hi[start : start + values.shape[0]] = high
        kernel_lo[start : start + values.shape[0]] = low

    for copy in state_in:
        copy.wait()
    for tap in range(TAPS):
        set_kernel(
            tap, 0, numerator[:, tap * channels : (tap + 1) * channels] / first_weight[0:1, 0:1]
        )

    def process(step, owner):
        signal = split(acts[step, owner])
        taps_out[...] = product((kernel_hi[...], kernel_lo[...]), signal, ((1,), (0,)))
        output = jnp.zeros((rows, pixels), jnp.float32)
        for tap in range(TAPS):
            value = taps_out[tap * padded : tap * padded + rows]
            moved = pltpu.roll(value, -tap_shift(tap) % pixels, 1) if tap_shift(tap) else value
            output += jnp.where(tap_mask(tap, pixels), moved, 0.0)
        residual = gap_rows[step, owner] + tap_scale * output
        for tap in range(TAPS):
            value = jnp.where(tap_mask(tap, pixels), residual, 0.0)
            if tap_shift(tap):
                value = pltpu.roll(value, tap_shift(tap) % pixels, 1)
            high, low = split(value)
            res_hi[tap * padded : tap * padded + rows] = high
            res_lo[tap * padded : tap * padded + rows] = low
        total[...] += product((res_hi[...], res_lo[...]), signal, ((1,), (1,)))

    for step in range(STEPS):
        total[...] = jnp.zeros(total.shape, jnp.float32)

        def visit(k, _, step=step):
            away = (k + 1) // 2
            owner = jnp.where(lax.rem(k, 2) == 1, me - away, me + away)

            @pl.when((owner >= 0) & (owner < shards))
            def _():
                @pl.when(owner < me)
                def _():
                    acts_copy(step, owner, True).wait_recv()

                    @pl.when(me < shards - 1)
                    def _():
                        acts_copy(step, owner, True).start()

                    if step < STEPS - 1:

                        @pl.when(owner == 0)
                        def _():
                            send_own(step + 1, True)

                @pl.when(owner > me)
                def _():
                    acts_copy(step, owner, False).wait_recv()

                    @pl.when(me > 0)
                    def _():
                        acts_copy(step, owner, False).start()

                    if step < STEPS - 1:

                        @pl.when(owner == shards - 1)
                        def _():
                            send_own(step + 1, False)

                @pl.when(owner != me)
                def _():
                    gap_arrival(step, owner).wait_recv()

                process(step, owner)

            return 0

        lax.fori_loop(0, 2 * shards - 1, visit, 0)

        if step > 0:
            for part in range(rows // chunk):
                push_copy(step - 1, part).wait_recv()
        order = list(range(rows // chunk))
        for part in order[-1:] + order[:-1]:
            span = slice(part * chunk, (part + 1) * chunk)
            for tap in range(TAPS):
                cut = slice(tap * channels, (tap + 1) * channels)
                start = tap * padded + part * chunk
                gradient = total[start : start + chunk] * (tap_scale / replica_batch)
                old = (momentum if step == 0 else momentum_out)[span, cut]
                new = momentum_decay * old + gradient
                momentum_out[span, cut] = new
                base = (numerator if step == 0 else numerator_out)[span, cut]
                half = 0.5 * (base - step_size * new)
                outbox[step, span, cut] = half
                fresh = half + (arrived if step == 0 else inbox)[span, cut]
                numerator_out[span, cut] = fresh
                if step < STEPS - 1:
                    set_kernel(tap, part * chunk, fresh / second_weight[0:1, 0:1])
            if detour and step == STEPS - 1 and part == last_part:

                @pl.when(at_end)
                def _():
                    to_relay().start()

                @pl.when(jnp.logical_not(at_end))
                def _():
                    push_copy(STEPS - 1, last_part).start()

            else:
                push_copy(step, part).start()

    if detour:

        @pl.when(beside_end)
        def _():
            to_relay().wait_recv()
            from_relay().start()

    for step in range(STEPS):
        weight_copy(step).wait_recv()
    weight_out[...] = (0.5 * second_weight + weight_box[1, 0])[0:1, 0:1]
    pending_weight_out[...] = weight_box[1, 1][0:1, 0:1]
    for step in range(STEPS):
        weight_copy(step).wait_send()
        for part in range(rows // chunk):
            if detour and step == STEPS - 1 and part == last_part:

                @pl.when(at_end)
                def _():
                    to_relay().wait_send()

                @pl.when(jnp.logical_not(at_end))
                def _():
                    push_copy(STEPS - 1, last_part).wait_send()

                @pl.when(beside_end)
                def _():
                    from_relay().wait_send()

            else:
                push_copy(step, part).wait_send()
            if step == STEPS - 1:
                push_copy(step, part).wait_recv()

        def drain(owner, _, step=step):
            @pl.when((owner <= me) & (me < shards - 1))
            def _():
                acts_copy(step, owner, True).wait_send()

            @pl.when((owner >= me) & (me > 0))
            def _():
                acts_copy(step, owner, False).wait_send()

            @pl.when(owner != me)
            def _():
                gap_copy(step, owner).wait_send()

            return 0

        lax.fori_loop(0, shards, drain, 0)


def deliver(first_in, second_in, third_in, first_out, second_out, third_out, sems):
    pairs = ((first_in, first_out), (second_in, second_out), (third_in, third_out))
    copies = [
        pltpu.make_async_copy(source, target, sems.at[k])
        for k, (source, target) in enumerate(pairs)
    ]
    for copy in copies:
        copy.start()
    for copy in copies:
        copy.wait()


def solution(mesh):
    reps, shards = mesh.shape["rep"], mesh.shape["fsdp"]

    def local(
        latents, gaussian, stamps, numerator, momentum, push_weight, arrived, arrived_weight
    ):
        steps, samples, channels, pixels = latents.shape
        rows, columns = numerator.shape[1:]
        assert samples == 1 and steps == STEPS
        padded = -(-rows // 16) * 16
        chunk = 16 if rows % 16 == 0 else rows
        parts = rows // chunk
        vmem = pl.BlockSpec(memory_space=pltpu.VMEM)
        dma = pltpu.SemaphoreType.DMA
        state = pltpu.VMEM((rows, columns), jnp.float32)
        one = jax.ShapeDtypeStruct((1, 1), jnp.float32)
        outs = pl.pallas_call(
            functools.partial(body, (reps, shards, padded, chunk)),
            out_shape=(state, state, one, state, one),
            in_specs=[pl.BlockSpec(memory_space=pltpu.SMEM), vmem, vmem]
            + [pl.BlockSpec(memory_space=pl.ANY)] * 5,
            out_specs=(vmem,) * 5,
            scratch_shapes=[
                pltpu.VMEM((steps, channels, pixels), jnp.float32),
                pltpu.VMEM((steps, channels, pixels), jnp.float32),
                pltpu.VMEM((rows, columns), jnp.float32),
                pltpu.VMEM((rows, columns), jnp.float32),
                pltpu.VMEM((rows, columns), jnp.float32),
                dma((2 * steps + 3,)),
                pltpu.VMEM((steps, shards, channels, pixels), jnp.float32),
                pltpu.VMEM((steps, shards, rows, pixels), jnp.float32),
                pltpu.VMEM((steps, shards, rows, pixels), jnp.float32),
                pltpu.VMEM((TAPS * padded, channels), jnp.bfloat16),
                pltpu.VMEM((TAPS * padded, channels), jnp.bfloat16),
                pltpu.VMEM((TAPS * padded, pixels), jnp.bfloat16),
                pltpu.VMEM((TAPS * padded, pixels), jnp.bfloat16),
                pltpu.VMEM((TAPS * padded, channels), jnp.float32),
                pltpu.VMEM((TAPS * padded, pixels), jnp.float32),
                pltpu.VMEM((steps, rows, columns), jnp.float32),
                pltpu.VMEM((rows, columns), jnp.float32),
                pltpu.VMEM((2, steps, 8, 128), jnp.float32),
                pltpu.VMEM((chunk, columns), jnp.float32),
                dma((3,)),
                dma((2, steps, shards)),
                dma((steps, shards)),
                dma((steps, shards)),
                dma((steps, shards)),
                dma((steps, parts)),
                dma((steps, parts)),
                dma((steps,)),
                dma((steps,)),
            ],
            compiler_params=pltpu.CompilerParams(
                collective_id=0, has_side_effects=True, vmem_limit_bytes=56 * 1024 * 1024
            ),
        )(
            stamps.reshape(steps),
            push_weight.reshape(1, 1),
            arrived_weight.reshape(1, 1),
            latents.reshape(steps, channels, pixels),
            gaussian.reshape(steps, channels, pixels),
            numerator[0],
            momentum[0],
            arrived[0],
        )
        stored = jax.ShapeDtypeStruct((rows, columns), jnp.float32)
        results = pl.pallas_call(
            deliver,
            out_shape=(stored,) * 3,
            in_specs=[vmem] * 3,
            out_specs=(pl.BlockSpec(memory_space=pl.ANY),) * 3,
            scratch_shapes=[dma((3,))],
            compiler_params=pltpu.CompilerParams(vmem_limit_bytes=48 * 1024 * 1024),
        )(outs[0], outs[1], outs[3])
        return (results[0][None], results[1][None], outs[2][0], results[2][None], outs[4][0])

    in_specs = (
        P(None, ("rep", "fsdp"), None, None),
        P(None, ("rep", "fsdp"), None, None),
        P(None, ("rep", "fsdp")),
        P("rep", "fsdp", None),
        P("rep", "fsdp", None),
        P("rep"),
        P("rep", "fsdp", None),
        P("rep"),
    )
    out_specs = (
        P("rep", "fsdp", None),
        P("rep", "fsdp", None),
        P("rep"),
        P("rep", "fsdp", None),
        P("rep"),
    )
    return jax.shard_map(local, mesh=mesh, in_specs=in_specs, out_specs=out_specs, check_vma=False)
```
